32 devices in a mesh: chain: 4 (over y, core), dp: 8 (over z, x).
Axes of the slice: x: 2, y: 2, z: 4, core: 2. Of those that a mesh axis runs over, the one named last changes fastest.
Arguments:
- train_features: float32 [256, 8, 8, 64], P('dp'), may hold values from -20 to 20
- train_labels: int32 [256], P('dp'), may hold values from 0 to 9
- test_features: float32 [512, 8, 8, 64], P('dp'), may hold values from -6 to 6
- conv_first: float32 [4, 9, 64, 64], P('chain'), may hold values from -0.25 to 0.25
- conv_second: float32 [4, 9, 64, 64], P('chain'), may hold values from -0.25 to 0.25
- norm_params: float32 [4, 6, 64], P('chain'), may hold values from -3 to 3
- head_weight: float32 [4, 64, 10], P('chain'), may hold values from -0.75 to 0.75
- head_bias: float32 [4, 10], P('chain'), may hold values from -3 to 3
- mom_first: float32 [4, 9, 64, 64], P('chain'), may hold values from -6 to 6
- mom_second: float32 [4, 9, 64, 64], P('chain'), may hold values from -6 to 6
- mom_norm: float32 [4, 6, 64], P('chain'), may hold values from -6 to 6
- mom_head: float32 [4, 64, 10], P('chain'), may hold values from -6 to 6
- mom_bias: float32 [4, 10], P('chain'), may hold values from -6 to 6
- step_size: float32 [4], P('chain'), may hold values from 0.001 to 0.003
Outputs:
- predictive: float32 [512, 10], P('dp')
- hamiltonians: float32 [4, 2], P('chain')
- potentials: float32 [4, 2], P('chain')
- forces: float32 [4, 2, 9, 64, 64], P('chain', None, None, 'dp')
The draws below stay inside these ranges and needn't reach their ends.
All inputs are finite; a program needn't handle non-finite values.
Results may differ from the reference program's by a relative error of at most 0.0003.
Values sent between devices are 32-bit elements; how exact they have to be, the bound alone decides.
A program may use at most 128 MiB of HBM per device.

```python
import math
import jax
import jax.numpy as jnp
from jax import lax

CH = 64
CLASSES = 10
SIDE = 8
TAPS = 9
IMAGES = 256
TESTS = 512
CHAINS = 4


def draw_train_features(key, part):
    first_key = jax.random.fold_in(key, 11)
    place = jnp.arange(IMAGES, dtype=jnp.float32) / jnp.float32(max(IMAGES - 1, 1))
    scale = jnp.exp(place * math.log(4.0))
    values = jax.random.truncated_normal(first_key, -4.0, 4.0, (IMAGES, SIDE, SIDE, CH), jnp.float32)
    return values * scale[:, None, None, None]


def with_ends(drawn, stream_key, low, largest):
    longest = drawn.shape.index(max(drawn.shape))
    spots = []
    for shift in (0, 1):
        where = [jax.random.randint(jax.random.fold_in(stream_key, axis), (), 0, length) for axis, length in enumerate(drawn.shape)]
        where[longest] = (where[longest] + shift) % drawn.shape[longest]
        spots.append(tuple(where))
    return drawn.at[spots[0]].set(low).at[spots[1]].set(largest)


def shard_levels(key, dims, cuts, smallest, largest):
    def one(dim, parts):
        steps = jax.random.uniform(jax.random.fold_in(jax.random.fold_in(key, 6), dim), (parts,), jnp.float32, smallest / len(cuts), largest / len(cuts))
        return jnp.repeat(jnp.exp(steps), dims[dim] // parts).reshape((-1,) + (1,) * (len(dims) - dim - 1))

    factor_of = one(*cuts[0])
    for cut in cuts[1:]:
        factor_of = factor_of * one(*cut)
    return factor_of


def noise(own_key, extent, deviation, reach, cuts=(), kind=jnp.bfloat16):
    loudness = shard_levels(own_key, extent, cuts, -0.22, 0.18) if cuts else 1.0
    entries = jax.random.normal(own_key, extent, jnp.float32) * deviation * loudness
    return jnp.minimum(jnp.maximum(entries, -reach), reach).astype(kind)


def setup_inputs(seed: int = 0) -> dict:
    arg_keys = jax.random.split(jax.random.key(seed), 15)
    train_features = draw_train_features(jax.random.fold_in(arg_keys[14], 71), 0)
    train_labels = with_ends(jax.random.randint(arg_keys[1], (IMAGES,), 0, CLASSES), jax.random.fold_in(arg_keys[1], 1), 0, CLASSES - 1).astype(jnp.int32)
    test_features = noise(arg_keys[2], (TESTS, SIDE, SIDE, CH), 1.0, 6.0, ((0, 8),), jnp.float32)
    conv_first = noise(arg_keys[3], (CHAINS, TAPS, CH, CH), (TAPS * CH) ** -0.5, 0.25, ((0, 4),), jnp.float32)
    conv_second = noise(arg_keys[4], (CHAINS, TAPS, CH, CH), (TAPS * CH) ** -0.5, 0.25, ((0, 4),), jnp.float32)
    norm_params = noise(arg_keys[5], (CHAINS, 6, CH), 0.5, 3.0, ((0, 4),), jnp.float32)
    head_weight = noise(arg_keys[6], (CHAINS, CH, CLASSES), CH ** -0.5, 0.75, ((0, 4),), jnp.float32)
    head_bias = noise(arg_keys[7], (CHAINS, CLASSES), 0.5, 3.0, ((0, 4),), jnp.float32)
    mom_first = noise(arg_keys[8], (CHAINS, TAPS, CH, CH), 1.0, 6.0, ((0, 4),), jnp.float32)
    mom_second = noise(arg_keys[9], (CHAINS, TAPS, CH, CH), 1.0, 6.0, ((0, 4),), jnp.float32)
    mom_norm = noise(arg_keys[10], (CHAINS, 6, CH), 1.0, 6.0, ((0, 4),), jnp.float32)
    mom_head = noise(arg_keys[11], (CHAINS, CH, CLASSES), 1.0, 6.0, ((0, 4),), jnp.float32)
    mom_bias = noise(arg_keys[12], (CHAINS, CLASSES), 1.0, 6.0, ((0, 4),), jnp.float32)
    step_size = jnp.clip(jnp.exp(math.log(0.003) - 1.09861225 * jax.random.uniform(arg_keys[13], (CHAINS,), jnp.float32) ** shard_levels(arg_keys[13], (CHAINS,), ((0, 4),), -0.2, 0.2)), 0.001, 0.003)
    return {"train_features": train_features, "train_labels": train_labels, "test_features": test_features, "conv_first": conv_first, "conv_second": conv_second, "norm_params": norm_params, "head_weight": head_weight, "head_bias": head_bias, "mom_first": mom_first, "mom_second": mom_second, "mom_norm": mom_norm, "mom_head": mom_head, "mom_bias": mom_bias, "step_size": step_size}


highest = lax.Precision.HIGHEST
epsilon = 1e-06

def conv_layer(inputs, kernel):
    height = inputs.shape[1]
    breadth = inputs.shape[2]
    padded = jnp.pad(inputs, ((0, 0), (1, 1), (1, 1), (0, 0)))
    total = jnp.zeros(inputs.shape[:3] + (kernel.shape[2],), jnp.float32)
    for offset in range(9):
        row_off = offset // 3
        col_off = offset % 3
        window = padded[:, row_off:row_off + height, col_off:col_off + breadth, :]
        total = total + jnp.einsum('bhwc,cd->bhwd', window, kernel[offset], precision=highest)
    return total

def normalize(values, gain, shift):
    moment = lax.optimization_barrier(jnp.mean(values * values, axis=(1, 2), keepdims=True))
    return values * lax.rsqrt(moment + epsilon) * gain + shift

def network(params, features):
    kernel_one, kernel_two, norms, weights, biases = params
    hidden = jnp.maximum(normalize(conv_layer(features, kernel_one), norms[0], norms[1]), norms[2])
    branch = normalize(conv_layer(hidden, kernel_two), norms[3], norms[4])
    joined = jnp.maximum(features + branch, norms[5])
    pooled = lax.optimization_barrier(jnp.mean(joined, axis=(1, 2)))
    return jnp.dot(pooled, weights, precision=highest) + biases

def cross_sum(params, features, labels):
    logits = network(params, features)
    onehot = (labels[:, None] == jnp.arange(logits.shape[1], dtype=jnp.int32)[None, :]).astype(jnp.float32)
    return jnp.sum(jax.nn.logsumexp(logits, axis=1) - lax.optimization_barrier(jnp.sum(onehot * logits, axis=1)))

def squares_half(params):
    total = jnp.float32(0.0)
    for tensor in params:
        total = total + 0.5 * jnp.sum(tensor * tensor)
    return total

def reference(train_features, train_labels, test_features, conv_first, conv_second, norm_params, head_weight, head_bias, mom_first, mom_second, mom_norm, mom_head, mom_bias, step_size):

    def potential(position):
        return cross_sum(position, train_features, train_labels) + squares_half(position)
    value_grad = jax.value_and_grad(potential)

    def one_chain(chain_args):
        position = tuple(chain_args[0:5])
        start_mom = tuple(chain_args[5:10])
        stride = chain_args[10]
        energy_start, grad_start = value_grad(position)
        momentum = tuple((mom_val - 0.5 * stride * grad_val for mom_val, grad_val in zip(start_mom, grad_start)))
        position = tuple((pos_val + stride * mom_val for pos_val, mom_val in zip(position, momentum)))
        unused, grad_middle = value_grad(position)
        momentum = tuple((mom_val - stride * grad_val for mom_val, grad_val in zip(momentum, grad_middle)))
        position = tuple((pos_val + stride * mom_val for pos_val, mom_val in zip(position, momentum)))
        energy_end, grad_end = value_grad(position)
        momentum = tuple((mom_val - 0.5 * stride * grad_val for mom_val, grad_val in zip(momentum, grad_end)))
        pair = jnp.stack([energy_start + squares_half(start_mom), energy_end + squares_half(momentum)])
        pot_pair = jnp.stack([energy_start, energy_end])
        force_one = 0.5 * grad_start[0] + grad_middle[0] + 0.5 * grad_end[0]
        force_two = 0.5 * grad_start[1] + grad_middle[1] + 0.5 * grad_end[1]
        probs = jax.nn.softmax(network(position, test_features), axis=-1)
        return (probs, pair, pot_pair, jnp.stack([force_one, force_two]))
    probs_all, pairs, pot_pairs, force_all = lax.map(one_chain, (conv_first, conv_second, norm_params, head_weight, head_bias, mom_first, mom_second, mom_norm, mom_head, mom_bias, step_size))
    predictive = lax.optimization_barrier(jnp.sum(probs_all, axis=0)) / CHAINS
    return (predictive, pairs, pot_pairs, force_all)
```

```python
import functools

import jax
import jax.numpy as jnp
from jax import lax
from jax.experimental import pallas as pl
from jax.experimental.pallas import tpu as pltpu
from jax.sharding import PartitionSpec as P

MESH = pl.DeviceIdType.MESH
HIGHEST = lax.Precision.HIGHEST
EPS = 1e-6
CH = 64
TAPS = 9
SMALL = 24
F32 = jnp.float32
BF16 = jnp.bfloat16


def split(value):
    high = value.astype(BF16)
    return high, (value - high.astype(F32)).astype(BF16)


def mm(left, right):
    return jnp.dot(left, right, preferred_element_type=F32)


def put_weights(ref, taps):
    zero = jnp.zeros((CH, CH), F32)
    for a in range(3):
        mine = taps[3 * a : 3 * a + 3]
        left = jnp.concatenate(mine + [zero], axis=0)
        right = jnp.concatenate([zero] + mine, axis=0)
        high, low = split(jnp.concatenate([left, right], axis=1))
        ref[256 * a : 256 * a + 256, 0:128] = high
        ref[256 * a : 256 * a + 256, 128:256] = low


def put_padded(hs, ls, value, images):
    rows, width = value.shape
    edge = jnp.zeros((rows, CH), F32)
    high, low = split(jnp.concatenate([edge, value, edge], axis=1))
    block = jnp.zeros((images, width + 2 * CH), BF16)
    for ref, val in ((hs, high), (ls, low)):
        ref[0:images, :] = block
        ref[images : images + rows, :] = val
        ref[images + rows : 2 * images + rows, :] = block


def conv(hs, ls, weights, images):
    rows = hs.shape[0] - 2 * images
    outs = []
    for p in range((hs.shape[1] - 128) // 128):
        def window(ref):
            return jnp.concatenate(
                [ref[a * images : a * images + rows, 128 * p : 128 * p + 256] for a in range(3)], axis=1
            )
        both = mm(window(hs), weights[...])
        outs.append(both[:, :128] + both[:, 128:] + mm(window(ls), weights[:, :128]))
    return jnp.concatenate(outs, axis=1)


def kernel_grad(value, hs, ls, images):
    rows, width = value.shape
    high, low = split(value.T)
    totals = [None] * 3
    for p in range(width // 128):
        part_high = high[128 * p : 128 * p + 128]
        stacked = jnp.concatenate([part_high, low[128 * p : 128 * p + 128]], axis=0)
        for a in range(3):
            start = (2 - a) * images
            both = mm(stacked, hs[start : start + rows, 128 * p : 128 * p + 256])
            both = both[:128] + both[128:]
            both = both + mm(part_high, ls[start : start + rows, 128 * p : 128 * p + 256])
            totals[a] = both if totals[a] is None else totals[a] + both
    grads = []
    for a in range(3):
        for b in range(3):
            grads.append(
                totals[a][0:64, (2 - b) * 64 : (3 - b) * 64] + totals[a][64:128, (3 - b) * 64 : (4 - b) * 64]
            )
    return grads


def over_columns(value):
    width = value.shape[1]
    shift = width // 2
    while shift >= CH:
        value = value + pltpu.roll(value, shift, 1)
        shift //= 2
    return value


def over_pixels(value, images):
    total = value[0:images]
    for h in range(1, value.shape[0] // images):
        total = total + value[h * images : (h + 1) * images]
    return over_columns(total)


def spread(value, rows):
    return jnp.concatenate([value] * (rows // value.shape[0]), axis=0)


def wide(row, width):
    return jnp.concatenate([row] * (width // CH), axis=1)


def above(value, bound):
    return jnp.where(value > bound, 1.0, jnp.where(value == bound, 0.5, 0.0))


def load_taps(theta, columns):
    shards = theta.shape[0]
    per = CH // shards
    return [
        jnp.concatenate([theta[s, t * per : (t + 1) * per, columns] for s in range(shards)], axis=0)
        for t in range(TAPS)
    ]


def forward(x, theta, small, images, refs):
    hs, ls, ys, yl, w_one, w_two = refs
    rows, width = x.shape
    pixels = rows // images * (width // CH)
    taps_two = load_taps(theta, slice(64, 128))
    put_weights(w_one, load_taps(theta, slice(0, 64)))
    put_weights(w_two, taps_two)
    norms = [wide(small[k : k + 1, 0:64], width) for k in range(6)]
    put_padded(hs, ls, x, images)
    c1 = conv(hs, ls, w_one, images)
    r1 = spread(lax.rsqrt(over_pixels(c1 * c1, images) / pixels + EPS), rows)
    u1 = c1 * r1
    v1 = u1 * norms[0] + norms[1]
    y = jnp.maximum(v1, norms[2])
    put_padded(ys, yl, y, images)
    c2 = conv(ys, yl, w_two, images)
    r2 = spread(lax.rsqrt(over_pixels(c2 * c2, images) / pixels + EPS), rows)
    u2 = c2 * r2
    t = x + (u2 * norms[3] + norms[4])
    pooled = (over_pixels(jnp.maximum(t, norms[5]), images) / pixels)[:, 0:64]
    head = small[8:24, 0:64]
    logits = lax.dot_general(
        pooled, head, (((1,), (1,)), ((), ())), precision=HIGHEST, preferred_element_type=F32
    ) + small[6:7, 0:16]
    return norms, taps_two, r1, u1, v1, y, r2, u2, t, pooled, head, logits


def soft(logits, classes):
    valid = lax.broadcasted_iota(jnp.int32, logits.shape, 1) < classes
    top = jnp.max(jnp.where(valid, logits, -jnp.inf), axis=1, keepdims=True)
    powers = jnp.where(valid, jnp.exp(jnp.where(valid, logits - top, 0.0)), 0.0)
    total = jnp.sum(powers, axis=1, keepdims=True)
    return powers / total, top + jnp.log(total)


def grad_kernel(classes, x_ref, hot_ref, theta, small, out, hs, ls, ys, yl, w_one, w_two, w_back):
    x = x_ref[...]
    rows, width = x.shape
    images = hot_ref.shape[0]
    pixels = rows // images * (width // CH)
    norms, taps_two, r1, u1, v1, y, r2, u2, t, pooled, head, logits = forward(
        x, theta, small, images, (hs, ls, ys, yl, w_one, w_two)
    )
    hot = hot_ref[...]
    probs, lse = soft(logits, classes)
    cross = jnp.sum(lse - jnp.sum(hot * logits, axis=1, keepdims=True), axis=0, keepdims=True)
    dlog = probs - hot
    dhead = lax.dot_general(dlog, pooled, (((0,), (0,)), ((), ())), precision=HIGHEST, preferred_element_type=F32)
    dbias = jnp.sum(dlog, axis=0, keepdims=True)
    dpool = jnp.dot(dlog, head, precision=HIGHEST, preferred_element_type=F32) / pixels
    dout = spread(wide(dpool, width), rows)
    keep = above(t, norms[5])
    dz = dout * keep

    def by_channel(value):
        return over_columns(jnp.sum(value, axis=0, keepdims=True))[:, 0:64]

    dn5 = by_channel(dout - dz)
    dn4 = by_channel(dz)
    dn3 = by_channel(dz * u2)
    du = dz * norms[3]
    g2 = r2 * (du - u2 * spread(over_pixels(du * u2, images) / pixels, rows))
    put_weights(w_back, [tap.T for tap in reversed(taps_two)])
    put_padded(hs, ls, g2, images)
    grads_two = kernel_grad(y, hs, ls, images)
    dy = conv(hs, ls, w_back, images)
    dv = dy * above(v1, norms[2])
    dn2 = by_channel(dy - dv)
    dn1 = by_channel(dv)
    dn0 = by_channel(dv * u1)
    du = dv * norms[0]
    g1 = r1 * (du - u1 * spread(over_pixels(du * u1, images) / pixels, rows))
    put_padded(ys, yl, g1, images)
    grads_one = kernel_grad(x, ys, yl, images)
    shards = out.shape[0]
    per = CH // shards
    base = TAPS * per
    tail = jnp.zeros((1, 112), F32)
    half = jnp.zeros((1, 64), F32)
    block = jnp.concatenate(
        [jnp.concatenate([row, half], axis=1) for row in (dn0, dn1, dn2, dn3, dn4, dn5)]
        + [jnp.concatenate([dbias, tail], axis=1), jnp.broadcast_to(cross, (1, 128))]
        + [jnp.concatenate([dhead, jnp.zeros((16, 64), F32)], axis=1)],
        axis=0,
    )
    for tap in range(TAPS):
        both = jnp.concatenate([grads_one[tap], grads_two[tap]], axis=1)
        for s in range(shards):
            out[s, tap * per : (tap + 1) * per, :] = both[s * per : (s + 1) * per]
    for s in range(shards):
        out[s, base : base + SMALL, :] = block


def test_kernel(classes, x_ref, theta, small, out, hs, ls, ys, yl, w_one, w_two):
    images = out.shape[0]
    logits = forward(x_ref[...], theta, small, images, (hs, ls, ys, yl, w_one, w_two))[-1]
    out[...] = jnp.concatenate([soft(logits, classes)[0], jnp.zeros((images, 112), F32)], axis=1)


def compute_scratch(rows, width, images, backward):
    padded = pltpu.VMEM((rows + 2 * images, width + 128), BF16)
    return [padded] * 4 + [pltpu.VMEM((768, 256), BF16)] * (3 if backward else 2)


def vmem():
    return pl.BlockSpec(memory_space=pltpu.VMEM)


def greet(axes):
    barrier = pltpu.get_barrier_semaphore()
    count = 0
    for axis in axes:
        n = lax.axis_size(axis)
        me = lax.axis_index(axis)
        for k in range(1, n):
            pl.semaphore_signal(barrier, inc=1, device_id={axis: lax.rem(me + k, n)}, device_id_type=MESH)
        count += n - 1
    pl.semaphore_wait(barrier, count)


def send_all(axis, source, slot, send_sem, recv_sem):
    n = lax.axis_size(axis)
    me = lax.axis_index(axis)
    copies = []
    for k in range(1, n):
        peer = lax.rem(me + k, n)
        copy = pltpu.make_async_remote_copy(
            src_ref=source(peer), dst_ref=slot(me), send_sem=send_sem.at[k], recv_sem=recv_sem.at[k],
            device_id={axis: peer}, device_id_type=MESH,
        )
        copy.start()
        copies.append(copy)
    return copies


def finish(copies):
    for copy in copies:
        copy.wait_recv()
    for copy in copies:
        copy.wait_send()


def in_order(ref):
    total = ref[0]
    for s in range(1, ref.shape[0]):
        total = total + ref[s]
    return total


def move_kernel(factor, step, grads, theta, mom, small, small_mom,
                theta_all, new_mom, new_small, new_small_mom, force, sums, got, mine, send_a, recv_a, send_b, recv_b):
    me = lax.axis_index("dp")
    base = mom.shape[0]
    h = step[0]
    greet(("dp",))
    copies = send_all("dp", lambda s: grads.at[s], lambda s: got.at[s], send_a, recv_a)
    got[me] = grads[me]
    finish(copies)
    total = in_order(got)
    grad = total[0:base] + theta[me]
    mom_next = mom[...] - (factor * h) * grad
    mine[...] = theta[me] + h * mom_next
    copies = send_all("dp", lambda s: mine, lambda s: theta_all.at[s], send_b, recv_b)
    theta_all[me] = mine[...]
    new_mom[...] = mom_next
    force[...] = grad
    sums[...] = total[base : base + SMALL]
    real = lax.broadcasted_iota(jnp.int32, (SMALL, 128), 0) != 7
    small_grad = jnp.where(real, total[base : base + SMALL] + small[...], 0.0)
    small_next = small_mom[...] - (factor * h) * small_grad
    new_small_mom[...] = small_next
    new_small[...] = small[...] + h * small_next
    finish(copies)


def last_kernel(step, grads, theta, mom, small, small_mom, force_a, force_b, probs,
                force, sums, kinetic, mean, got, mine, parts, seen, send_a, recv_a, send_b, recv_b, send_c, recv_c):
    me = lax.axis_index("dp")
    chain = lax.axis_index("chain")
    base = mom.shape[0]
    h = step[0]
    greet(("dp", "chain"))
    copies = send_all("dp", lambda s: grads.at[s], lambda s: got.at[s], send_a, recv_a)
    others = send_all("chain", lambda s: probs, lambda s: seen.at[s], send_c, recv_c)
    got[me] = grads[me]
    seen[chain] = probs[...]
    finish(copies)
    total = in_order(got)
    grad = total[0:base] + theta[me]
    mom_next = mom[...] - (0.5 * h) * grad
    mine[...] = jnp.broadcast_to(jnp.sum(mom_next * mom_next, axis=0, keepdims=True), (8, 128))
    copies = send_all("dp", lambda s: mine, lambda s: parts.at[s], send_b, recv_b)
    parts[me] = mine[...]
    force[...] = 0.5 * force_a[...] + force_b[...] + 0.5 * grad
    sums[...] = total[base : base + SMALL]
    real = lax.broadcasted_iota(jnp.int32, (SMALL, 128), 0) != 7
    small_grad = jnp.where(real, total[base : base + SMALL] + small[...], 0.0)
    small_next = small_mom[...] - (0.5 * h) * small_grad
    finish(others)
    mean[...] = in_order(seen) / lax.axis_size("chain")
    finish(copies)
    kinetic[...] = in_order(parts)[0:1] + jnp.sum(small_next * small_next, axis=0, keepdims=True)


def pack_small(norms, head, bias):
    classes = head.shape[1]
    top = jnp.pad(norms, ((0, 0), (0, 64)))
    row = jnp.pad(bias[None, :], ((0, 1), (0, 128 - classes)))
    return jnp.concatenate([top, row, jnp.pad(head.T, ((0, 16 - classes), (0, 64)))], axis=0)


def pack_maps(features):
    images, height, width, channels = features.shape
    return jnp.reshape(jnp.transpose(features, (1, 0, 2, 3)), (height * images, width * channels))


def shards(train_features, train_labels, test_features, conv_first, conv_second, norm_params, head_weight, head_bias,
           mom_first, mom_second, mom_norm, mom_head, mom_bias, step_size):
    n = lax.axis_size("dp")
    chains = lax.axis_size("chain")
    me = lax.axis_index("dp")
    per = CH // n
    base = TAPS * per
    classes = head_weight.shape[2]
    images = train_features.shape[0]
    tests = test_features.shape[0]

    def pack(first, second):
        joined = jnp.concatenate([first, second], axis=2)
        return jnp.transpose(jnp.reshape(joined, (TAPS, n, per, 128)), (1, 0, 2, 3)).reshape(n, base, 128)

    theta = pack(conv_first[0], conv_second[0])
    mom_all = pack(mom_first[0], mom_second[0])
    mom = lax.dynamic_index_in_dim(mom_all, me, 0, keepdims=False)
    small = pack_small(norm_params[0], head_weight[0], head_bias[0])
    small_mom = pack_small(mom_norm[0], mom_head[0], mom_bias[0])
    train = pack_maps(train_features)
    test = pack_maps(test_features)
    hot = (train_labels[:, None] == jnp.arange(16, dtype=jnp.int32)[None, :]).astype(F32)

    def shape(*dims):
        return jax.ShapeDtypeStruct(dims, F32)

    def evaluate(theta, small):
        return pl.pallas_call(
            functools.partial(grad_kernel, classes),
            out_shape=shape(n, base + SMALL, 128),
            in_specs=[vmem()] * 4,
            out_specs=vmem(),
            scratch_shapes=compute_scratch(train.shape[0], train.shape[1], images, True),
            compiler_params=pltpu.CompilerParams(vmem_limit_bytes=50 << 20),
            name="gradient",
        )(train, hot, theta, small)

    pairs = [pltpu.SemaphoreType.DMA((n,))] * 2

    def move(index, factor, grads, theta, mom, small, small_mom):
        return pl.pallas_call(
            functools.partial(move_kernel, factor),
            out_shape=[shape(n, base, 128), shape(base, 128), shape(SMALL, 128), shape(SMALL, 128),
                       shape(base, 128), shape(SMALL, 128)],
            in_specs=[pl.BlockSpec(memory_space=pltpu.SMEM)] + [vmem()] * 5,
            out_specs=[vmem()] * 6,
            scratch_shapes=[pltpu.VMEM((n, base + SMALL, 128), F32), pltpu.VMEM((base, 128), F32)] + pairs + pairs,
            compiler_params=pltpu.CompilerParams(collective_id=index, has_side_effects=True),
            name="move%d" % index,
        )(step_size, grads, theta, mom, small, small_mom)

    start = 0.5 * (jnp.sum(theta * theta) + jnp.sum(small * small))
    start_kinetic = 0.5 * (jnp.sum(mom_all * mom_all) + jnp.sum(small_mom * small_mom))
    grads = evaluate(theta, small)
    theta, mom, small, small_mom, force_a, sums_a = move(0, 0.5, grads, theta, mom, small, small_mom)
    grads = evaluate(theta, small)
    theta, mom, small, small_mom, force_b, _ = move(1, 1.0, grads, theta, mom, small, small_mom)
    grads = evaluate(theta, small)
    probs = pl.pallas_call(
        functools.partial(test_kernel, classes),
        out_shape=shape(tests, 128),
        in_specs=[vmem()] * 3,
        out_specs=vmem(),
        scratch_shapes=compute_scratch(test.shape[0], test.shape[1], tests, False),
        compiler_params=pltpu.CompilerParams(vmem_limit_bytes=50 << 20),
        name="predict",
    )(test, theta, small)
    force, sums_b, kinetic, mean = pl.pallas_call(
        last_kernel,
        out_shape=[shape(base, 128), shape(SMALL, 128), shape(1, 128), shape(tests, 128)],
        in_specs=[pl.BlockSpec(memory_space=pltpu.SMEM)] + [vmem()] * 8,
        out_specs=[vmem()] * 4,
        scratch_shapes=[pltpu.VMEM((n, base + SMALL, 128), F32), pltpu.VMEM((8, 128), F32),
                        pltpu.VMEM((n, 8, 128), F32), pltpu.VMEM((chains, tests, 128), F32)]
        + pairs + pairs + [pltpu.SemaphoreType.DMA((chains,))] * 2,
        compiler_params=pltpu.CompilerParams(collective_id=2, has_side_effects=True),
        name="finish",
    )(step_size, grads, theta, mom, small, small_mom, force_a, force_b, probs)
    energy_start = sums_a[7, 0] + start
    energy_end = sums_b[7, 0] + 0.5 * (jnp.sum(theta * theta) + jnp.sum(small * small))
    potentials = jnp.stack([energy_start, energy_end])[None]
    pair = potentials + jnp.stack([start_kinetic, 0.5 * jnp.sum(kinetic)])[None]
    both = jnp.reshape(force, (TAPS, per, 2, 64))
    forces = jnp.transpose(both, (2, 0, 1, 3))[None]
    return mean[:, :classes], pair, potentials, forces


def solution(mesh):
    placed = (
        P("dp", None, None, None),
        P("dp"),
        P("dp", None, None, None),
        P("chain", None, None, None),
        P("chain", None, None, None),
        P("chain", None, None),
        P("chain", None, None),
        P("chain", None),
        P("chain", None, None, None),
        P("chain", None, None, None),
        P("chain", None, None),
        P("chain", None, None),
        P("chain", None),
        P("chain"),
    )
    return jax.shard_map(
        shards,
        mesh=mesh,
        in_specs=placed,
        out_specs=(
            P("dp", None),
            P("chain", None),
            P("chain", None),
            P("chain", None, None, "dp", None),
        ),
        check_vma=False,
    )
```

```python
import functools

import jax
import jax.numpy as jnp
from jax import lax
from jax.experimental import pallas as pl
from jax.experimental.pallas import tpu as pltpu
from jax.sharding import PartitionSpec as P

MESH = pl.DeviceIdType.MESH
HIGHEST = lax.Precision.HIGHEST
EPS = 1e-6
CH = 64
TAPS = 9
SMALL = 16
F32 = jnp.float32
BF16 = jnp.bfloat16


def split(value):
    high = value.astype(BF16)
    return high, (value - high.astype(F32)).astype(BF16)


def mm(left, right):
    return jnp.dot(left, right, preferred_element_type=F32)


def put_weights(ref, taps):
    zero = jnp.zeros((CH, CH), F32)
    for a in range(3):
        mine = taps[3 * a : 3 * a + 3]
        left = jnp.concatenate(mine + [zero], axis=0)
        right = jnp.concatenate([zero] + mine, axis=0)
        high, low = split(jnp.concatenate([left, right], axis=1))
        ref[256 * a : 256 * a + 256, 0:128] = high
        ref[256 * a : 256 * a + 256, 128:256] = low


def put_padded(hs, ls, value, images):
    rows, width = value.shape
    edge = jnp.zeros((rows, CH), F32)
    high, low = split(jnp.concatenate([edge, value, edge], axis=1))
    block = jnp.zeros((images, width + 2 * CH), BF16)
    for ref, val in ((hs, high), (ls, low)):
        ref[0:images, :] = block
        ref[images : images + rows, :] = val
        ref[images + rows : 2 * images + rows, :] = block


def conv(hs, ls, weights, images):
    rows = hs.shape[0] - 2 * images
    outs = []
    for p in range((hs.shape[1] - 128) // 128):
        def window(ref):
            return jnp.concatenate(
                [ref[a * images : a * images + rows, 128 * p : 128 * p + 256] for a in range(3)], axis=1
            )
        both = mm(window(hs), weights[...])
        outs.append(both[:, :128] + both[:, 128:] + mm(window(ls), weights[:, :128]))
    return jnp.concatenate(outs, axis=1)


def kernel_grad(turned, hs, ls, images):
    high, low = turned
    width, rows = high.shape
    totals = [None] * 3
    for p in range(width // 128):
        part_high = high[128 * p : 128 * p + 128]
        stacked = jnp.concatenate([part_high, low[128 * p : 128 * p + 128]], axis=0)
        for a in range(3):
            start = (2 - a) * images
            both = mm(stacked, hs[start : start + rows, 128 * p : 128 * p + 256])
            both = both[:128] + both[128:]
            both = both + mm(part_high, ls[start : start + rows, 128 * p : 128 * p + 256])
            totals[a] = both if totals[a] is None else totals[a] + both
    grads = []
    for a in range(3):
        for b in range(3):
            grads.append(
                totals[a][0:64, (2 - b) * 64 : (3 - b) * 64] + totals[a][64:128, (3 - b) * 64 : (4 - b) * 64]
            )
    return grads


def over_columns(value):
    width = value.shape[1]
    shift = width // 2
    while shift >= CH:
        value = value + pltpu.roll(value, shift, 1)
        shift //= 2
    return value


def over_pixels(value, images):
    total = value[0:images]
    for h in range(1, value.shape[0] // images):
        total = total + value[h * images : (h + 1) * images]
    return over_columns(total)


def spread(value, rows):
    return jnp.concatenate([value] * (rows // value.shape[0]), axis=0)


def wide(row, width):
    return jnp.concatenate([row] * (width // CH), axis=1)


def above(value, bound):
    return jnp.where(value > bound, 1.0, jnp.where(value == bound, 0.5, 0.0))


def load_taps(theta, which):
    shards = theta.shape[0]
    per = CH // shards

    def tap(t):
        block = 8 if t == 8 else (t // 2 if which else 4 + t // 2)
        lane = 64 * (which if t == 8 else t % 2)
        return jnp.concatenate([theta[s, block * per : (block + 1) * per, lane : lane + 64] for s in range(shards)], axis=0)

    return [tap(t) for t in range(TAPS)]


def own_share(first, second, me, per):
    rows = pl.ds(pl.multiple_of(me * per, per), per)

    def pair(left, right):
        return jnp.concatenate([left, right], axis=1)

    blocks = [pair(second[0, 2 * i, rows, :], second[0, 2 * i + 1, rows, :]) for i in range(4)]
    blocks += [pair(first[0, 2 * i, rows, :], first[0, 2 * i + 1, rows, :]) for i in range(4)]
    return jnp.concatenate(blocks + [pair(first[0, 8, rows, :], second[0, 8, rows, :])], axis=0)


def head_rows(small):
    return jnp.concatenate([small[3:8, 0:64], small[3:8, 64:128], jnp.zeros((6, 64), F32)], axis=0)


def small_block(norms, head, bias, loss):
    return jnp.concatenate(
        [
            jnp.concatenate([norms[0:3], norms[3:6]], axis=1),
            jnp.concatenate([head[0:5], head[5:10]], axis=1),
            jnp.concatenate([bias, jnp.zeros((1, 48), F32), loss], axis=1),
            jnp.zeros((7, 128), F32),
        ],
        axis=0,
    )


def pack_small(norms, head, bias, square):
    classes = head.shape[2]
    square[...] = jnp.zeros_like(square)
    square[0:64, 0:classes] = head[0]
    turned = square[...].T
    square[0:1, :] = jnp.zeros((1, 128), F32)
    square[0:1, 0:classes] = bias[...]
    return small_block(norms[0], turned[0:16, 0:64], square[0:1, 0:16], jnp.zeros((1, 64), F32))


def forward(x, taps_one, taps_two, small, images, refs):
    hs, ls, ys, yl, w_one, w_two = refs
    rows, width = x.shape
    pixels = rows // images * (width // CH)
    put_weights(w_one, taps_one)
    put_weights(w_two, taps_two)
    norms = [wide(small[k % 3 : k % 3 + 1, 64 * (k // 3) : 64 * (k // 3) + 64], width) for k in range(6)]
    c1 = conv(hs, ls, w_one, images)
    r1 = spread(lax.rsqrt(over_pixels(c1 * c1, images) / pixels + EPS), rows)
    u1 = c1 * r1
    v1 = u1 * norms[0] + norms[1]
    y = jnp.maximum(v1, norms[2])
    put_padded(ys, yl, y, images)
    c2 = conv(ys, yl, w_two, images)
    r2 = spread(lax.rsqrt(over_pixels(c2 * c2, images) / pixels + EPS), rows)
    u2 = c2 * r2
    t = x + (u2 * norms[3] + norms[4])
    pooled = (over_pixels(jnp.maximum(t, norms[5]), images) / pixels)[:, 0:64]
    head = head_rows(small)
    logits = lax.dot_general(
        pooled, head, (((1,), (1,)), ((), ())), precision=HIGHEST, preferred_element_type=F32
    ) + small[8:9, 0:16]
    return norms, r1, u1, v1, y, r2, u2, t, pooled, head, logits


def soft(logits, classes):
    valid = lax.broadcasted_iota(jnp.int32, logits.shape, 1) < classes
    top = jnp.max(jnp.where(valid, logits, -jnp.inf), axis=1, keepdims=True)
    powers = jnp.where(valid, jnp.exp(jnp.where(valid, logits - top, 0.0)), 0.0)
    total = jnp.sum(powers, axis=1, keepdims=True)
    return powers / total, top + jnp.log(total)


def gradient(classes, x, hot, taps_one, taps_two, small, refs, early, late, send_early, send_late):
    xs, xl, ys, yl, gs, gl, w_one, w_two, w_back, turned_high, turned_low = refs
    rows, width = x.shape
    images = hot.shape[0]
    pixels = rows // images * (width // CH)
    norms, r1, u1, v1, y, r2, u2, t, pooled, head, logits = forward(
        x, taps_one, taps_two, small, images, (xs, xl, ys, yl, w_one, w_two)
    )
    probs, lse = soft(logits, classes)
    cross = jnp.sum(lse - jnp.sum(hot * logits, axis=1, keepdims=True), axis=0, keepdims=True)
    dlog = probs - hot
    dhead = lax.dot_general(dlog, pooled, (((0,), (0,)), ((), ())), precision=HIGHEST, preferred_element_type=F32)
    dbias = jnp.sum(dlog, axis=0, keepdims=True)
    dpool = jnp.dot(dlog, head, precision=HIGHEST, preferred_element_type=F32) / pixels
    dout = spread(wide(dpool, width), rows)
    dz = dout * above(t, norms[5])

    def by_channel(value):
        return over_columns(jnp.sum(value, axis=0, keepdims=True))[:, 0:64]

    dn5 = by_channel(dout - dz)
    dn4 = by_channel(dz)
    dn3 = by_channel(dz * u2)
    du = dz * norms[3]
    g2 = r2 * (du - u2 * spread(over_pixels(du * u2, images) / pixels, rows))
    put_padded(gs, gl, g2, images)
    grads_two = kernel_grad(split(y.T), gs, gl, images)
    shards = early.shape[0]
    per = CH // shards
    for i in range(4):
        both = jnp.concatenate([grads_two[2 * i], grads_two[2 * i + 1]], axis=1)
        for s in range(shards):
            early[s, i * per : (i + 1) * per, :] = both[s * per : (s + 1) * per]
    send_early()
    put_weights(w_back, [tap.T for tap in reversed(taps_two)])
    dy = conv(gs, gl, w_back, images)
    dv = dy * above(v1, norms[2])
    dn2 = by_channel(dy - dv)
    dn1 = by_channel(dv)
    dn0 = by_channel(dv * u1)
    du = dv * norms[0]
    g1 = r1 * (du - u1 * spread(over_pixels(du * u1, images) / pixels, rows))
    put_padded(ys, yl, g1, images)
    grads_one = kernel_grad((turned_high[...], turned_low[...]), ys, yl, images)
    block = small_block(
        jnp.concatenate([dn0, dn1, dn2, dn3, dn4, dn5], axis=0), dhead, dbias, jnp.broadcast_to(cross, (1, 64))
    )
    for i in range(5):
        both = jnp.concatenate([grads_one[2 * i], grads_two[8] if i == 4 else grads_one[2 * i + 1]], axis=1)
        for s in range(shards):
            late[s, i * per : (i + 1) * per, :] = both[s * per : (s + 1) * per]
    for s in range(shards):
        late[s, 5 * per : 5 * per + SMALL, :] = block
    send_late()


def greet(axes):
    barrier = pltpu.get_barrier_semaphore()
    count = 0
    for axis in axes:
        n = lax.axis_size(axis)
        me = lax.axis_index(axis)
        for k in range(1, n):
            pl.semaphore_signal(barrier, inc=1, device_id={axis: lax.rem(me + k, n)}, device_id_type=MESH)
        count += n - 1
    return lambda: pl.semaphore_wait(barrier, count)


def send_all(axis, source, slot, send_sem, recv_sem):
    n = lax.axis_size(axis)
    me = lax.axis_index(axis)
    copies = []
    for k in range(1, n):
        peer = lax.rem(me + k, n)
        copy = pltpu.make_async_remote_copy(
            src_ref=source(peer), dst_ref=slot(me), send_sem=send_sem.at[k], recv_sem=recv_sem.at[k],
            device_id={axis: peer}, device_id_type=MESH,
        )
        copy.start()
        copies.append(copy)
    return copies


def finish(copies):
    for copy in copies:
        copy.wait_recv()
    for copy in copies:
        copy.wait_send()


def in_order(ref):
    total = ref[0]
    for s in range(1, ref.shape[0]):
        total = total + ref[s]
    return total


def all_sum(value):
    while value.ndim > 2:
        value = jnp.sum(value, axis=0)
    return jnp.sum(jnp.sum(value, axis=0, keepdims=True), axis=1, keepdims=True)


def square_sum(value):
    return all_sum(value * value)


def whole_kernel(classes, step, x_ref, hot_ref, test_ref, first, second, norms, head, bias,
                 mom_first, mom_second, mom_norm, mom_head, mom_bias,
                 mean, hamiltonians, potentials, forces,
                 xs, xl, ys, yl, gs, gl, w_one, w_two, w_back, turned_high, turned_low, ts, tl, us, ul,
                 square, early, late, got_early, got_late, theta_all, small_all, share, small_mom, mom, mine, part,
                 parts, probs_own, seen, send_a, recv_a, send_b, recv_b, send_c, recv_c, send_d, recv_d, send_e, recv_e):
    n = lax.axis_size("dp")
    me = lax.axis_index("dp")
    chain = lax.axis_index("chain")
    per = CH // n
    h = step[0]
    arrived = greet(("dp", "chain"))
    x = x_ref[...]
    images = hot_ref.shape[0]
    tests = mean.shape[0]
    put_padded(xs, xl, x, images)
    turned_high[...], turned_low[...] = split(x.T)
    share[...] = own_share(first, second, me, per)
    mom[...] = own_share(mom_first, mom_second, me, per)
    small_all[0] = pack_small(norms, head, bias, square)
    small_mom[...] = pack_small(mom_norm, mom_head, mom_bias, square)
    refs = (xs, xl, ys, yl, gs, gl, w_one, w_two, w_back, turned_high, turned_low)
    line = lax.broadcasted_iota(jnp.int32, (SMALL, 128), 0)
    lane = lax.broadcasted_iota(jnp.int32, (SMALL, 128), 1)
    real = jnp.logical_or(line != 8, lane < 64)
    arrived()
    taps_one = [first[0, t] for t in range(TAPS)]
    taps_two = [second[0, t] for t in range(TAPS)]
    force = None
    for stage, factor in enumerate((0.5, 1.0, 0.5)):
        small = small_all.at[stage]
        copies = []

        def send_early():
            copies.extend(send_all("dp", lambda s: early.at[s], lambda s: got_early.at[stage, s],
                                   send_a.at[stage], recv_a.at[stage]))

        def send_late():
            copies.extend(send_all("dp", lambda s: late.at[s], lambda s: got_late.at[stage, s],
                                   send_b.at[stage], recv_b.at[stage]))

        gradient(classes, x, hot_ref[...], taps_one, taps_two, small, refs, early, late, send_early, send_late)
        got_early[stage, me] = early[me]
        got_late[stage, me] = late[me]
        if stage == 0:
            theta_squares = square_sum(first[0]) + square_sum(second[0]) + square_sum(small[...])
            mom_squares = square_sum(mom_first[0]) + square_sum(mom_second[0]) + square_sum(small_mom[...])
        if stage == 2:
            xt = test_ref[...]
            put_padded(ts, tl, xt, tests)
            logits = forward(xt, taps_one, taps_two, small, tests, (ts, tl, us, ul, w_one, w_two))[-1]
            probs_own[...] = jnp.concatenate([soft(logits, classes)[0], jnp.zeros((tests, 112), F32)], axis=1)
            others = send_all("chain", lambda s: probs_own, lambda s: seen.at[s], send_d, recv_d)
            seen[chain] = probs_own[...]
            share_squares = jnp.sum(share[...] * share[...], axis=0, keepdims=True)
        finish(copies)
        late_sum = in_order(got_late.at[stage])
        grad = jnp.concatenate([in_order(got_early.at[stage]), late_sum[0 : 5 * per]], axis=0) + share[...]
        sums = late_sum[5 * per : 5 * per + SMALL]
        mom_next = mom[...] - (factor * h) * grad
        small_grad = jnp.where(real, sums + small[...], 0.0)
        small_next = small_mom[...] - (factor * h) * small_grad
        weight = 0.5 if stage != 1 else 1.0
        force = weight * grad if force is None else force + weight * grad
        if stage < 2:
            mine[...] = share[...] + h * mom_next
            copies = send_all("dp", lambda s: mine, lambda s: theta_all.at[stage, s], send_c.at[stage], recv_c.at[stage])
            theta_all[stage, me] = mine[...]
            share[...] = mine[...]
            mom[...] = mom_next
            small_mom[...] = small_next
            small_all[stage + 1] = small[...] + h * small_next
            if stage == 0:
                energy_start = sums[8:9, 64:65] + 0.5 * theta_squares
            finish(copies)
            taps_one = load_taps(theta_all.at[stage], 0)
            taps_two = load_taps(theta_all.at[stage], 1)
    part[...] = jnp.concatenate(
        [jnp.sum(mom_next * mom_next, axis=0, keepdims=True), share_squares, jnp.zeros((6, 128), F32)], axis=0
    )
    copies = send_all("dp", lambda s: part, lambda s: parts.at[s], send_e, recv_e)
    parts[me] = part[...]
    for i in range(4):
        rows = slice(i * per, (i + 1) * per)
        for which, at in ((1, slice(i * per, (i + 1) * per)), (0, slice((4 + i) * per, (5 + i) * per))):
            forces[0, which, 2 * i] = force[at, 0:64]
            forces[0, which, 2 * i + 1] = force[at, 64:128]
    forces[0, 0, 8] = force[8 * per : 9 * per, 0:64]
    forces[0, 1, 8] = force[8 * per : 9 * per, 64:128]
    finish(others)
    mean[...] = (in_order(seen) / lax.axis_size("chain"))[:, 0:classes]
    small_squares = square_sum(small_all[2])
    kinetic_small = square_sum(small_next)
    finish(copies)
    both = in_order(parts)
    energy_end = sums[8:9, 64:65] + 0.5 * (all_sum(both[1:2]) + small_squares)
    pot = jnp.concatenate([energy_start, energy_end], axis=1)
    potentials[...] = pot
    hamiltonians[...] = pot + 0.5 * jnp.concatenate([mom_squares, all_sum(both[0:1]) + kinetic_small], axis=1)


def pack_maps(features):
    images, height, width, channels = features.shape
    return jnp.reshape(jnp.transpose(features, (1, 0, 2, 3)), (height * images, width * channels))


def vmem():
    return pl.BlockSpec(memory_space=pltpu.VMEM)


def shards(train_features, train_labels, test_features, *rest):
    n = lax.axis_size("dp")
    chains = lax.axis_size("chain")
    per = CH // n
    classes = rest[3].shape[2]
    images = train_features.shape[0]
    tests = test_features.shape[0]
    train = pack_maps(train_features)
    test = pack_maps(test_features)
    hot = (train_labels[:, None] == jnp.arange(16, dtype=jnp.int32)[None, :]).astype(F32)
    rows, width = train.shape
    small_maps = [pltpu.VMEM((rows + 2 * images, width + 128), BF16)] * 6
    large_maps = [pltpu.VMEM((test.shape[0] + 2 * tests, width + 128), BF16)] * 4

    def shape(*dims):
        return jax.ShapeDtypeStruct(dims, F32)

    def buffer(*dims):
        return pltpu.VMEM(dims, F32)

    def pair(*dims):
        return [pltpu.SemaphoreType.DMA(dims)] * 2

    return pl.pallas_call(
        functools.partial(whole_kernel, classes),
        out_shape=(shape(tests, classes), shape(1, 2), shape(1, 2), shape(1, 2, TAPS, per, 64)),
        in_specs=[pl.BlockSpec(memory_space=pltpu.SMEM)] + [vmem()] * 13,
        out_specs=[vmem()] * 4,
        scratch_shapes=small_maps + [pltpu.VMEM((768, 256), BF16)] * 3 + [pltpu.VMEM((width, rows), BF16)] * 2
        + large_maps
        + [buffer(128, 128), buffer(n, 4 * per, 128), buffer(n, 5 * per + SMALL, 128),
           buffer(3, n, 4 * per, 128), buffer(3, n, 5 * per + SMALL, 128), buffer(2, n, 9 * per, 128),
           buffer(3, SMALL, 128), buffer(9 * per, 128), buffer(SMALL, 128), buffer(9 * per, 128), buffer(9 * per, 128),
           buffer(8, 128), buffer(n, 8, 128), buffer(tests, 128), buffer(chains, tests, 128)]
        + pair(3, n) + pair(3, n) + pair(2, n) + pair(chains) + pair(n),
        compiler_params=pltpu.CompilerParams(
            collective_id=0, has_side_effects=True, vmem_limit_bytes=56 << 20
        ),
        name="leapfrog",
    )(rest[-1], train, hot, test, *rest[:-1])


def solution(mesh):
    placed = (
        P("dp", None, None, None),
        P("dp"),
        P("dp", None, None, None),
        P("chain", None, None, None),
        P("chain", None, None, None),
        P("chain", None, None),
        P("chain", None, None),
        P("chain", None),
        P("chain", None, None, None),
        P("chain", None, None, None),
        P("chain", None, None),
        P("chain", None, None),
        P("chain", None),
        P("chain"),
    )
    return jax.shard_map(
        shards,
        mesh=mesh,
        in_specs=placed,
        out_specs=(
            P("dp", None),
            P("chain", None),
            P("chain", None),
            P("chain", None, None, "dp", None),
        ),
        check_vma=False,
    )
```

```python
import functools

import jax
import jax.numpy as jnp
from jax import lax
from jax.experimental import pallas as pl
from jax.experimental.pallas import tpu as pltpu
from jax.sharding import PartitionSpec as P

MESH = pl.DeviceIdType.MESH
HIGHEST = lax.Precision.HIGHEST
EPS = 1e-6
CH = 64
TAPS = 9
SMALL = 16
F32 = jnp.float32
BF16 = jnp.bfloat16


def split(value):
    high = value.astype(BF16)
    return high, (value - high.astype(F32)).astype(BF16)


def mm(left, right):
    return jnp.dot(left, right, preferred_element_type=F32)


def put_weights(ref, taps):
    zero = jnp.zeros((CH, CH), F32)
    for a in range(3):
        mine = taps[3 * a : 3 * a + 3]
        left = jnp.concatenate(mine + [zero], axis=0)
        right = jnp.concatenate([zero] + mine, axis=0)
        high, low = split(jnp.concatenate([left, right], axis=1))
        ref[256 * a : 256 * a + 256, 0:128] = high
        ref[256 * a : 256 * a + 256, 128:256] = low


def put_padded(hs, ls, value, images):
    rows, width = value.shape
    edge = jnp.zeros((rows, CH), F32)
    high, low = split(jnp.concatenate([edge, value, edge], axis=1))
    block = jnp.zeros((images, width + 2 * CH), BF16)
    for ref, val in ((hs, high), (ls, low)):
        ref[0:images, :] = block
        ref[images : images + rows, :] = val
        ref[images + rows : 2 * images + rows, :] = block


def conv(hs, ls, weights, images):
    rows = hs.shape[0] - 2 * images
    outs = []
    for p in range((hs.shape[1] - 128) // 128):
        def window(ref):
            return jnp.concatenate(
                [ref[a * images : a * images + rows, 128 * p : 128 * p + 256] for a in range(3)], axis=1
            )
        both = mm(window(hs), weights[...])
        outs.append(both[:, :128] + both[:, 128:] + mm(window(ls), weights[:, :128]))
    return jnp.concatenate(outs, axis=1)


def kernel_grad(turned, hs, ls, images):
    high, low = turned
    width, rows = high.shape
    totals = [None] * 3
    for p in range(width // 128):
        part_high = high[128 * p : 128 * p + 128]
        stacked = jnp.concatenate([part_high, low[128 * p : 128 * p + 128]], axis=0)
        for a in range(3):
            start = (2 - a) * images
            both = mm(stacked, hs[start : start + rows, 128 * p : 128 * p + 256])
            both = both[:128] + both[128:]
            both = both + mm(part_high, ls[start : start + rows, 128 * p : 128 * p + 256])
            totals[a] = both if totals[a] is None else totals[a] + both
    grads = []
    for a in range(3):
        for b in range(3):
            grads.append(
                totals[a][0:64, (2 - b) * 64 : (3 - b) * 64] + totals[a][64:128, (3 - b) * 64 : (4 - b) * 64]
            )
    return grads


def over_columns(value):
    width = value.shape[1]
    shift = width // 2
    while shift >= CH:
        value = value + pltpu.roll(value, shift, 1)
        shift //= 2
    return value


def over_pixels(value, images):
    total = value[0:images]
    for h in range(1, value.shape[0] // images):
        total = total + value[h * images : (h + 1) * images]
    return over_columns(total)


def spread(value, rows):
    return jnp.concatenate([value] * (rows // value.shape[0]), axis=0)


def wide(row, width):
    return jnp.concatenate([row] * (width // CH), axis=1)


def above(value, bound):
    return jnp.where(value > bound, 1.0, jnp.where(value == bound, 0.5, 0.0))


def load_taps(theta, which):
    shards = theta.shape[0]
    per = CH // shards

    def tap(t):
        block = 8 if t == 8 else (t // 2 if which else 4 + t // 2)
        lane = 64 * (which if t == 8 else t % 2)
        return jnp.concatenate([theta[s, block * per : (block + 1) * per, lane : lane + 64] for s in range(shards)], axis=0)

    return [tap(t) for t in range(TAPS)]


def own_share(first, second, me, per):
    rows = pl.ds(pl.multiple_of(me * per, per), per)

    def pair(left, right):
        return jnp.concatenate([left, right], axis=1)

    blocks = [pair(second[0, 2 * i, rows, :], second[0, 2 * i + 1, rows, :]) for i in range(4)]
    blocks += [pair(first[0, 2 * i, rows, :], first[0, 2 * i + 1, rows, :]) for i in range(4)]
    return jnp.concatenate(blocks + [pair(first[0, 8, rows, :], second[0, 8, rows, :])], axis=0)


def head_rows(small):
    return jnp.concatenate([small[3:8, 0:64], small[3:8, 64:128], jnp.zeros((6, 64), F32)], axis=0)


def small_block(norms, head, bias, loss):
    return jnp.concatenate(
        [
            jnp.concatenate([norms[0:3], norms[3:6]], axis=1),
            jnp.concatenate([head[0:5], head[5:10]], axis=1),
            jnp.concatenate([bias, jnp.zeros((1, 48), F32), loss], axis=1),
            jnp.zeros((7, 128), F32),
        ],
        axis=0,
    )


def pack_small(norms, head, bias, row):
    classes = head.shape[0]
    zero = jnp.zeros((1, 64), F32)
    row[...] = jnp.zeros_like(row)
    row[0:1, 0:classes] = bias[...]
    lines = [head[k] for k in range(classes)] + [zero] * (16 - classes)
    return small_block(
        jnp.concatenate([norms[k] for k in range(6)], axis=0), jnp.concatenate(lines, axis=0), row[0:1, 0:16], zero
    )


def forward(x, taps_one, taps_two, small, images, refs):
    hs, ls, ys, yl, w_one, w_two = refs
    rows, width = x.shape
    pixels = rows // images * (width // CH)
    put_weights(w_one, taps_one)
    put_weights(w_two, taps_two)
    norms = [wide(small[k % 3 : k % 3 + 1, 64 * (k // 3) : 64 * (k // 3) + 64], width) for k in range(6)]
    c1 = conv(hs, ls, w_one, images)
    r1 = spread(lax.rsqrt(over_pixels(c1 * c1, images) / pixels + EPS), rows)
    u1 = c1 * r1
    v1 = u1 * norms[0] + norms[1]
    y = jnp.maximum(v1, norms[2])
    put_padded(ys, yl, y, images)
    c2 = conv(ys, yl, w_two, images)
    r2 = spread(lax.rsqrt(over_pixels(c2 * c2, images) / pixels + EPS), rows)
    u2 = c2 * r2
    t = x + (u2 * norms[3] + norms[4])
    pooled = (over_pixels(jnp.maximum(t, norms[5]), images) / pixels)[:, 0:64]
    head = head_rows(small)
    logits = lax.dot_general(
        pooled, head, (((1,), (1,)), ((), ())), precision=HIGHEST, preferred_element_type=F32
    ) + small[8:9, 0:16]
    return norms, r1, u1, v1, y, r2, u2, t, pooled, head, logits


def soft(logits, classes):
    valid = lax.broadcasted_iota(jnp.int32, logits.shape, 1) < classes
    top = jnp.max(jnp.where(valid, logits, -jnp.inf), axis=1, keepdims=True)
    powers = jnp.where(valid, jnp.exp(jnp.where(valid, logits - top, 0.0)), 0.0)
    total = jnp.sum(powers, axis=1, keepdims=True)
    return powers / total, top + jnp.log(total)


def gradient(classes, x, hot, taps_one, taps_two, small, refs, early, late, send_early, send_late):
    xs, xl, ys, yl, gs, gl, w_one, w_two, w_back, turned_high, turned_low = refs
    rows, width = x.shape
    images = hot.shape[0]
    pixels = rows // images * (width // CH)
    norms, r1, u1, v1, y, r2, u2, t, pooled, head, logits = forward(
        x, taps_one, taps_two, small, images, (xs, xl, ys, yl, w_one, w_two)
    )
    probs, lse = soft(logits, classes)
    cross = jnp.sum(lse - jnp.sum(hot * logits, axis=1, keepdims=True), axis=0, keepdims=True)
    dlog = probs - hot
    dhead = lax.dot_general(dlog, pooled, (((0,), (0,)), ((), ())), precision=HIGHEST, preferred_element_type=F32)
    dbias = jnp.sum(dlog, axis=0, keepdims=True)
    dpool = jnp.dot(dlog, head, precision=HIGHEST, preferred_element_type=F32) / pixels
    dout = spread(wide(dpool, width), rows)
    dz = dout * above(t, norms[5])

    def by_channel(value):
        return over_columns(jnp.sum(value, axis=0, keepdims=True))[:, 0:64]

    dn5 = by_channel(dout - dz)
    dn4 = by_channel(dz)
    dn3 = by_channel(dz * u2)
    du = dz * norms[3]
    g2 = r2 * (du - u2 * spread(over_pixels(du * u2, images) / pixels, rows))
    put_padded(gs, gl, g2, images)
    grads_two = kernel_grad(split(y.T), gs, gl, images)
    shards = early.shape[0]
    per = CH // shards
    for i in range(4):
        both = jnp.concatenate([grads_two[2 * i], grads_two[2 * i + 1]], axis=1)
        for s in range(shards):
            early[s, i * per : (i + 1) * per, :] = both[s * per : (s + 1) * per]
    send_early()
    put_weights(w_back, [tap.T for tap in reversed(taps_two)])
    dy = conv(gs, gl, w_back, images)
    dv = dy * above(v1, norms[2])
    dn2 = by_channel(dy - dv)
    dn1 = by_channel(dv)
    dn0 = by_channel(dv * u1)
    du = dv * norms[0]
    g1 = r1 * (du - u1 * spread(over_pixels(du * u1, images) / pixels, rows))
    put_padded(ys, yl, g1, images)
    grads_one = kernel_grad((turned_high[...], turned_low[...]), ys, yl, images)
    block = small_block(
        jnp.concatenate([dn0, dn1, dn2, dn3, dn4, dn5], axis=0), dhead, dbias, jnp.broadcast_to(cross, (1, 64))
    )
    for i in range(5):
        both = jnp.concatenate([grads_one[2 * i], grads_two[8] if i == 4 else grads_one[2 * i + 1]], axis=1)
        for s in range(shards):
            late[s, i * per : (i + 1) * per, :] = both[s * per : (s + 1) * per]
    for s in range(shards):
        late[s, 5 * per : 5 * per + SMALL, :] = block
    send_late()


def greet(axes):
    barrier = pltpu.get_barrier_semaphore()
    count = 0
    for axis in axes:
        n = lax.axis_size(axis)
        me = lax.axis_index(axis)
        for k in range(1, n):
            pl.semaphore_signal(barrier, inc=1, device_id={axis: lax.rem(me + k, n)}, device_id_type=MESH)
        count += n - 1
    return lambda: pl.semaphore_wait(barrier, count)


def send_all(axis, source, slot, send_sem, recv_sem):
    n = lax.axis_size(axis)
    me = lax.axis_index(axis)
    copies = []
    for k in sorted(range(1, n), key=lambda k: -min(k, n - k)):
        peer = lax.rem(me + k, n)
        copy = pltpu.make_async_remote_copy(
            src_ref=source(peer), dst_ref=slot(me), send_sem=send_sem.at[k], recv_sem=recv_sem.at[k],
            device_id={axis: peer}, device_id_type=MESH,
        )
        copy.start()
        copies.append(copy)
    return copies


def finish(copies):
    for copy in copies:
        copy.wait_recv()
    for copy in copies:
        copy.wait_send()


def in_order(ref):
    total = ref[0]
    for s in range(1, ref.shape[0]):
        total = total + ref[s]
    return total


def all_sum(value):
    while value.ndim > 2:
        value = jnp.sum(value, axis=0)
    return jnp.sum(jnp.sum(value, axis=0, keepdims=True), axis=1, keepdims=True)


def square_sum(value):
    return all_sum(value * value)


def whole_kernel(classes, step, x_ref, label_ref, test_ref, first, second, norms, head, bias,
                 mom_first, mom_second, mom_norm, mom_head, mom_bias,
                 mean, hamiltonians, potentials, forces,
                 xs, xl, ys, yl, gs, gl, w_one, w_two, w_back, turned_high, turned_low, ts, tl, us, ul,
                 square, early, late, got_early, got_late, theta_all, small_all, share, small_mom, mom, mine, part,
                 parts, probs_own, seen, send_a, recv_a, send_b, recv_b, send_c, recv_c, send_d, recv_d, send_e, recv_e):
    n = lax.axis_size("dp")
    me = lax.axis_index("dp")
    chain = lax.axis_index("chain")
    per = CH // n
    h = step[0]
    arrived = greet(("dp", "chain"))
    x = x_ref[...]
    images = label_ref.shape[1]
    spots = jnp.broadcast_to(label_ref[...], (128, images)) == lax.broadcasted_iota(jnp.int32, (128, images), 0)
    hot = jnp.where(spots, 1.0, 0.0).T[:, 0:16]
    tests = mean.shape[0]
    put_padded(xs, xl, x, images)
    turned_high[...], turned_low[...] = split(x.T)
    share[...] = own_share(first, second, me, per)
    mom[...] = own_share(mom_first, mom_second, me, per)
    small_all[0] = pack_small(norms, head, bias, square)
    small_mom[...] = pack_small(mom_norm, mom_head, mom_bias, square)
    refs = (xs, xl, ys, yl, gs, gl, w_one, w_two, w_back, turned_high, turned_low)
    line = lax.broadcasted_iota(jnp.int32, (SMALL, 128), 0)
    lane = lax.broadcasted_iota(jnp.int32, (SMALL, 128), 1)
    real = jnp.logical_or(line != 8, lane < 64)
    arrived()
    taps_one = [first[0, t] for t in range(TAPS)]
    taps_two = [second[0, t] for t in range(TAPS)]
    force = None
    for stage, factor in enumerate((0.5, 1.0, 0.5)):
        small = small_all.at[stage]
        copies = []

        def send_early():
            copies.extend(send_all("dp", lambda s: early.at[s], lambda s: got_early.at[stage, s],
                                   send_a.at[stage], recv_a.at[stage]))

        def send_late():
            copies.extend(send_all("dp", lambda s: late.at[s], lambda s: got_late.at[stage, s],
                                   send_b.at[stage], recv_b.at[stage]))

        gradient(classes, x, hot, taps_one, taps_two, small, refs, early, late, send_early, send_late)
        got_early[stage, me] = early[me]
        got_late[stage, me] = late[me]
        if stage == 0:
            theta_squares = square_sum(first[0]) + square_sum(second[0]) + square_sum(small[...])
            mom_squares = square_sum(mom_first[0]) + square_sum(mom_second[0]) + square_sum(small_mom[...])
        if stage == 2:
            xt = test_ref[...]
            put_padded(ts, tl, xt, tests)
            logits = forward(xt, taps_one, taps_two, small, tests, (ts, tl, us, ul, w_one, w_two))[-1]
            probs_own[...] = jnp.concatenate([soft(logits, classes)[0], jnp.zeros((tests, 112), F32)], axis=1)
            others = send_all("chain", lambda s: probs_own, lambda s: seen.at[s], send_d, recv_d)
            seen[chain] = probs_own[...]
            share_squares = jnp.sum(share[...] * share[...], axis=0, keepdims=True)
        finish(copies)
        late_sum = in_order(got_late.at[stage])
        grad = jnp.concatenate([in_order(got_early.at[stage]), late_sum[0 : 5 * per]], axis=0) + share[...]
        sums = late_sum[5 * per : 5 * per + SMALL]
        mom_next = mom[...] - (factor * h) * grad
        small_grad = jnp.where(real, sums + small[...], 0.0)
        small_next = small_mom[...] - (factor * h) * small_grad
        weight = 0.5 if stage != 1 else 1.0
        force = weight * grad if force is None else force + weight * grad
        if stage < 2:
            mine[...] = share[...] + h * mom_next
            copies = send_all("dp", lambda s: mine, lambda s: theta_all.at[stage, s], send_c.at[stage], recv_c.at[stage])
            theta_all[stage, me] = mine[...]
            share[...] = mine[...]
            mom[...] = mom_next
            small_mom[...] = small_next
            small_all[stage + 1] = small[...] + h * small_next
            if stage == 0:
                energy_start = sums[8:9, 64:65] + 0.5 * theta_squares
            finish(copies)
            taps_one = load_taps(theta_all.at[stage], 0)
            taps_two = load_taps(theta_all.at[stage], 1)
    part[...] = jnp.concatenate(
        [jnp.sum(mom_next * mom_next, axis=0, keepdims=True), share_squares, jnp.zeros((6, 128), F32)], axis=0
    )
    copies = send_all("dp", lambda s: part, lambda s: parts.at[s], send_e, recv_e)
    parts[me] = part[...]
    for i in range(4):
        rows = slice(i * per, (i + 1) * per)
        for which, at in ((1, slice(i * per, (i + 1) * per)), (0, slice((4 + i) * per, (5 + i) * per))):
            forces[0, which, 2 * i] = force[at, 0:64]
            forces[0, which, 2 * i + 1] = force[at, 64:128]
    forces[0, 0, 8] = force[8 * per : 9 * per, 0:64]
    forces[0, 1, 8] = force[8 * per : 9 * per, 64:128]
    finish(others)
    mean[...] = in_order(seen) / lax.axis_size("chain")
    small_squares = square_sum(small_all[2])
    kinetic_small = square_sum(small_next)
    finish(copies)
    both = in_order(parts)
    energy_end = sums[8:9, 64:65] + 0.5 * (all_sum(both[1:2]) + small_squares)
    pot = jnp.concatenate([energy_start, energy_end], axis=1)
    potentials[...] = pot
    hamiltonians[...] = pot + 0.5 * jnp.concatenate([mom_squares, all_sum(both[0:1]) + kinetic_small], axis=1)


def deliver_kernel(mean, hamiltonians, potentials, forces, mean_out, hamiltonians_out, potentials_out, forces_out):
    mean_out[...] = mean[...].T[0 : mean_out.shape[0]]
    hamiltonians_out[...] = hamiltonians[...]
    potentials_out[...] = potentials[...]
    forces_out[...] = forces[...]


def pack_maps(features):
    images, height, width, channels = features.shape
    return jnp.reshape(jnp.transpose(features, (1, 0, 2, 3)), (height * images, width * channels))


def vmem():
    return pl.BlockSpec(memory_space=pltpu.VMEM)


def shards(train_features, train_labels, test_features, *rest):
    n = lax.axis_size("dp")
    chains = lax.axis_size("chain")
    per = CH // n
    classes = rest[3].shape[2]
    images = train_features.shape[0]
    tests = test_features.shape[0]
    train = pack_maps(train_features)
    test = pack_maps(test_features)
    first, second, norms, head, bias, mom_first, mom_second, mom_norm, mom_head, mom_bias, step_size = rest

    def lead(array, order):
        return jnp.transpose(array, order)

    rest = (first, second, lead(norms, (1, 0, 2)), lead(head, (2, 0, 1)), bias,
            mom_first, mom_second, lead(mom_norm, (1, 0, 2)), lead(mom_head, (2, 0, 1)), mom_bias)
    rows, width = train.shape
    small_maps = [pltpu.VMEM((rows + 2 * images, width + 128), BF16)] * 6
    large_maps = [pltpu.VMEM((test.shape[0] + 2 * tests, width + 128), BF16)] * 4

    def shape(*dims):
        return jax.ShapeDtypeStruct(dims, F32)

    def buffer(*dims):
        return pltpu.VMEM(dims, F32)

    def pair(*dims):
        return [pltpu.SemaphoreType.DMA(dims)] * 2

    results = pl.pallas_call(
        functools.partial(whole_kernel, classes),
        out_shape=(shape(tests, 128), shape(1, 2), shape(1, 2), shape(1, 2, TAPS, per, 64)),
        in_specs=[pl.BlockSpec(memory_space=pltpu.SMEM)] + [vmem()] * 13,
        out_specs=[vmem()] * 4,
        scratch_shapes=small_maps + [pltpu.VMEM((768, 256), BF16)] * 3 + [pltpu.VMEM((width, rows), BF16)] * 2
        + large_maps
        + [buffer(8, 128), buffer(n, 4 * per, 128), buffer(n, 5 * per + SMALL, 128),
           buffer(3, n, 4 * per, 128), buffer(3, n, 5 * per + SMALL, 128), buffer(2, n, 9 * per, 128),
           buffer(3, SMALL, 128), buffer(9 * per, 128), buffer(SMALL, 128), buffer(9 * per, 128), buffer(9 * per, 128),
           buffer(8, 128), buffer(n, 8, 128), buffer(tests, 128), buffer(chains, tests, 128)]
        + pair(3, n) + pair(3, n) + pair(2, n) + pair(chains) + pair(n),
        compiler_params=pltpu.CompilerParams(
            collective_id=0, has_side_effects=True, vmem_limit_bytes=56 << 20
        ),
        name="leapfrog",
    )(step_size, train, jnp.reshape(train_labels, (1, images)), test, *rest)
    mean, hamiltonians, potentials, forces = pl.pallas_call(
        deliver_kernel,
        out_shape=(shape(classes, tests), shape(1, 2), shape(1, 2), shape(1, 2, TAPS, per, 64)),
        in_specs=[vmem()] * 4,
        out_specs=[vmem()] * 4,
        name="deliver",
    )(*results)
    return mean.T, hamiltonians, potentials, forces


def solution(mesh):
    placed = (
        P("dp", None, None, None),
        P("dp"),
        P("dp", None, None, None),
        P("chain", None, None, None),
        P("chain", None, None, None),
        P("chain", None, None),
        P("chain", None, None),
        P("chain", None),
        P("chain", None, None, None),
        P("chain", None, None, None),
        P("chain", None, None),
        P("chain", None, None),
        P("chain", None),
        P("chain"),
    )
    return jax.shard_map(
        shards,
        mesh=mesh,
        in_specs=placed,
        out_specs=(
            P("dp", None),
            P("chain", None),
            P("chain", None),
            P("chain", None, None, "dp", None),
        ),
        check_vma=False,
    )
```
